32 devices in a mesh: rows: 8 (over z, y), cols: 4 (over x, core).
Axes of the slice: x: 2, y: 2, z: 4, core: 2. Of those that a mesh axis runs over, the one named last changes fastest.
Arguments:
- right_sample: bfloat16 [2048, 320], P('rows', 'cols'), may hold values from -6 to 6
- left_sample: bfloat16 [2048, 320], P('rows', 'cols'), may hold values from -6 to 6
- updates: bfloat16 [8, 512, 512], P('rows'), may hold values from -0.25 to 0.25
- pattern: int32 [8, 4, 4], P('rows'), may hold values 0 or 1
- targets: int32 [8, 512], P('rows'), may hold values from 0 to 2047, as said below
- cluster_pos: int32 [2048], P('rows'), may hold values from 0 to 2047, as said below
- pivots: int32 [8, 128], P('rows'), may hold values from 0 to 255, as said below
Outputs:
- forward_out: float32 [2048, 320], P('rows', 'cols')
- transposed_out: float32 [2048, 320], P('rows', 'cols')
- interp: float32 [2048, 128], P('rows')
The draws below stay inside these ranges and needn't reach their ends.
Inputs may be any that keep to these rules, and one draw needn't show every extreme that they name: `targets`: the tile rows of one index of rows name at most 96 front rows held by any one index of rows; in every draw one index of rows receives exactly 96 from every index of rows. `cluster_pos`: A permutation; the 256 front rows of one index of rows take exactly 32 positions in the block of every index of rows. The pivots of one leaf are distinct.
All inputs are finite; a program needn't handle non-finite values. No bound on the sum of `pattern` on one device may be relied on, other than what follows from the above.
Results may differ from the reference program's by a relative error of at most 0.0003.
Values may be sent and summed in bfloat16 or wider, within the bound.
A program may use at most 64 MiB of HBM per device.

```python
import jax
import jax.numpy as jnp
from jax import lax

ROWS_DEV = 256
K = 320
BLOCK = 512
TILE = 128
CHILD_DEV = 1
LEAF = 256
RANK = 128
M = 2048
CHILDREN = 8
CAP = 96
LEAVES = 8
N_ROWS = 8


def draw_targets(key, part):
    row_total = CHILD_DEV * BLOCK
    busy_owner = jax.random.randint(jax.random.fold_in(key, 7), (), 0, N_ROWS)

    def single(device_key):
        key_slots, key_order, key_offsets = jax.random.split(device_key, 3)
        chosen = jax.random.permutation(key_slots, (N_ROWS - 1) * CAP)[:row_total - CAP]
        owners = chosen // CAP
        owners = owners + (owners >= busy_owner).astype(jnp.int32)
        owners = jnp.concatenate([jnp.full((CAP,), busy_owner, jnp.int32), owners.astype(jnp.int32)])
        owners = jax.random.permutation(key_order, owners)
        offsets = jax.random.randint(key_offsets, (row_total,), 0, ROWS_DEV)
        return owners * ROWS_DEV + offsets
    device_keys = jax.random.split(jax.random.fold_in(key, 11), N_ROWS)
    return jax.vmap(single)(device_keys).reshape(CHILDREN, BLOCK).astype(jnp.int32)


def draw_cluster_pos(key, part):
    group_size = ROWS_DEV // N_ROWS
    sigma_keys = jax.random.split(jax.random.fold_in(key, 21), N_ROWS)
    tau_keys = jax.random.split(jax.random.fold_in(key, 22), N_ROWS)
    sigma = jax.vmap(lambda each_key: jax.random.permutation(each_key, ROWS_DEV))(sigma_keys)
    tau = jax.vmap(lambda each_key: jax.random.permutation(each_key, ROWS_DEV))(tau_keys)
    target_dev = sigma // group_size
    within = sigma % group_size
    arrival = jnp.arange(N_ROWS, dtype=jnp.int32)[:, None] * group_size + within
    landing = tau[target_dev, arrival]
    return (target_dev * ROWS_DEV + landing).reshape(M).astype(jnp.int32)


def draw_pivots(key, part):
    leaf_keys = jax.random.split(jax.random.fold_in(key, 31), LEAVES)
    chosen = jax.vmap(lambda each_key: jax.random.permutation(each_key, LEAF)[:RANK])(leaf_keys)
    return chosen.astype(jnp.int32)


def set_ends(entries, key, low, largest):
    extent = entries.shape
    place = [jax.random.randint(jax.random.fold_in(key, axis), (), 0, extent[axis]) for axis in range(len(extent))]
    entries = entries.at[tuple(place)].set(low)
    longest = extent.index(max(extent))
    place[longest] = (place[longest] + 1) % extent[longest]
    return entries.at[tuple(place)].set(largest)


def steps_of(rng, shape, cuts, least, largest):
    def one(position, blocks):
        heights = jax.random.uniform(jax.random.fold_in(jax.random.fold_in(rng, 6), position), (blocks,), jnp.float32, least / len(cuts), largest / len(cuts))
        return jnp.repeat(jnp.exp(heights), shape[position] // blocks).reshape((-1,) + (1,) * (len(shape) - position - 1))

    loudness = one(*cuts[0])
    for cut in cuts[1:]:
        loudness = loudness * one(*cut)
    return loudness


def scatter_about(rng, dims, deviation, reach, cuts=(), kind=jnp.bfloat16):
    result = deviation * jax.random.normal(rng, dims, jnp.float32)
    if cuts:
        result = result * steps_of(rng, dims, cuts, -0.22, 0.18)
    return jnp.clip(result, -reach, reach).astype(kind)


def setup_inputs(seed: int = 0) -> dict:
    key_list = jax.random.split(jax.random.key(seed), 8)
    right_sample = scatter_about(key_list[0], (M, K), 1.0, 6.0, ((0, 8), (1, 4)))
    left_sample = scatter_about(key_list[1], (M, K), 1.0, 6.0, ((0, 8), (1, 4)))
    updates = scatter_about(key_list[2], (CHILDREN, BLOCK, BLOCK), BLOCK ** -0.5, 0.25, ((0, 8),))
    pattern = set_ends((jax.random.randint(key_list[3], (CHILDREN, BLOCK // TILE, BLOCK // TILE), 0, 4) < 3).astype(jnp.int32), jax.random.fold_in(key_list[3], 1), 0, 1)
    targets = draw_targets(jax.random.fold_in(key_list[7], 71), 0)
    cluster_pos = draw_cluster_pos(jax.random.fold_in(key_list[7], 71), 0)
    pivots = draw_pivots(jax.random.fold_in(key_list[7], 71), 0)
    return dict(right_sample=right_sample, left_sample=left_sample, updates=updates, pattern=pattern, targets=targets, cluster_pos=cluster_pos, pivots=pivots)


def reference(right_sample, left_sample, updates, pattern, targets, cluster_pos, pivots):
    both_samples = jnp.concatenate([right_sample, left_sample], axis=1)

    def add_child(front_rows, inputs):
        update, tile_mask, child_rows = inputs
        full_mask = jnp.repeat(jnp.repeat(tile_mask, TILE, axis=0), TILE, axis=1)
        masked = jnp.where(full_mask != 0, update, jnp.zeros_like(update))
        picked = both_samples[child_rows]
        forward_part = jnp.dot(masked.astype(jnp.float32), picked[:, :K].astype(jnp.float32), preferred_element_type=jnp.float32)
        transposed_part = jnp.dot(masked.T.astype(jnp.float32), picked[:, K:].astype(jnp.float32), preferred_element_type=jnp.float32)
        contrib = jnp.concatenate([forward_part, transposed_part], axis=1)
        return (front_rows.at[child_rows].add(contrib), None)
    front_rows, unused = lax.scan(add_child, jnp.zeros((M, 2 * K), jnp.float32), (updates, pattern, targets))
    clustered = jnp.zeros((M, 2 * K), jnp.float32).at[cluster_pos].set(front_rows)
    by_leaf = clustered.reshape(LEAVES, LEAF, 2 * K)
    skeleton = jnp.take_along_axis(by_leaf, pivots[:, :, None], axis=1)
    gram_sum = jnp.einsum('lrk,lsk->lrs', skeleton, skeleton, precision=lax.Precision.HIGHEST)
    cross_sum = jnp.einsum('lik,lsk->lis', by_leaf, skeleton, precision=lax.Precision.HIGHEST)
    gram = gram_sum / (2.0 * K) + jnp.eye(RANK, dtype=jnp.float32)[None]
    factor = jnp.linalg.cholesky(gram)
    solved = jax.scipy.linalg.cho_solve((factor, True), jnp.swapaxes(cross_sum / (2.0 * K), 1, 2))
    interp = jnp.swapaxes(solved, 1, 2).reshape(M, RANK)
    return (clustered[:, :K], clustered[:, K:], interp)
```

```python
import functools

import jax
import jax.numpy as jnp
from jax import lax
from jax.experimental import pallas as pl
from jax.experimental.pallas import tpu as pltpu
from jax.sharding import PartitionSpec as P

K = 320
LEAF = 256
RANK = 128
MESH = pl.DeviceIdType.MESH
F32 = jnp.float32
BF16 = jnp.bfloat16
QMAX = 32766.0
STEP = 4


def _up(value, unit):
    return -(-value // unit) * unit


def _dot(a, b, dims=((1,), (0,))):
    return lax.dot_general(a, b, (dims, ((), ())), preferred_element_type=F32)


TN = ((0,), (0,))
NT = ((1,), (1,))


def _iota(shape, dim):
    return lax.broadcasted_iota(jnp.int32, shape, dim)


def _split2(x):
    hi = x.astype(BF16)
    return hi, (x - hi.astype(F32)).astype(BF16)


def _digits(q):
    hi = jnp.floor(q * (1.0 / 256.0))
    return hi.astype(BF16), (q - 256.0 * hi).astype(BF16)


def _move_exact(sel, hi, lo, dims=((1,), (0,))):
    return 256.0 * _dot(sel, hi, dims) + _dot(sel, lo, dims)


def _encode(x, width):
    lane = _iota(x.shape, 1)
    top = jnp.max(jnp.where(lane < width, jnp.abs(x), 0.0), axis=1, keepdims=True)
    expo = jnp.clip(
        jnp.ceil(jnp.log(jnp.maximum(top, 1e-30)) * 1.4426950408889634 + 0.001), -96.0, 120.0
    )
    code = jnp.floor(x * (QMAX / jnp.exp2(expo)) + 0.5)
    return jnp.where(lane < width, code, jnp.where(lane == width, expo, 0.0))


def _decode(q, width):
    lane = _iota(q.shape, 1)
    scale = jnp.exp2(q[:, width : width + 1]) * (1.0 / QMAX)
    return jnp.where(lane < width, q * scale, 0.0)


def _folds(rows, lanes, width):
    stride = width + 2 - (lanes - 128)
    return max(f for f in range(1, 9)
               if f == 1 or (rows % f == 0 and (rows // f) % 16 == 0 and f * stride <= 128))


def _packed(rows, lanes, width):
    return rows * (lanes // 128 - 1) + rows // _folds(rows, lanes, width)


def _pack(x, width):
    rows, lanes = x.shape
    folds = _folds(rows, lanes, width)
    stride = width + 2 - (lanes - 128)
    part = rows // folds
    last = x[:, lanes - 128 :]
    tail = last[:part]
    for g in range(1, folds):
        tail = tail + pltpu.roll(last[g * part : (g + 1) * part], g * stride, axis=1)
    return jnp.concatenate([x[:, i : i + 128] for i in range(0, lanes - 128, 128)] + [tail], axis=0)


def _unpack(y, rows, lanes, width):
    folds = _folds(rows, lanes, width)
    stride = width + 2 - (lanes - 128)
    panels = lanes // 128 - 1
    tail = y[panels * rows :]
    pieces = [tail] + [pltpu.roll(tail, 128 - g * stride, axis=1) for g in range(1, folds)]
    last = jnp.concatenate(pieces, axis=0) if folds > 1 else tail
    last = jnp.where(_iota(last.shape, 1) < stride, last, 0.0)
    return jnp.concatenate([y[i * rows : (i + 1) * rows] for i in range(panels)] + [last], axis=1)


def _positions(row, count, span, stride):
    length = row.shape[1]
    rows8 = _up(count, 16)
    holder = _iota((rows8, length), 0)
    hot = (row >= holder * span) & (row < (holder + 1) * span)
    hot_f = hot.astype(F32)
    before = (_iota((length, length), 0) < _iota((length, length), 1)).astype(F32).astype(BF16)
    rank = _dot(hot_f.astype(BF16), before)
    slot = jnp.sum(hot_f * (rank + (holder * stride).astype(F32)), axis=0, keepdims=True)
    base = jnp.sum(hot_f * (holder * span).astype(F32), axis=0, keepdims=True)
    return slot.astype(jnp.int32), row - base.astype(jnp.int32)


def _order(count):
    return sorted(range(1, count), key=lambda o: (min(o, count - o), o))


def _each(count, body, far=False):
    if count <= 17:
        for o in _order(count)[:: -1 if far else 1]:
            body(o)
    else:
        lax.fori_loop(1, count, lambda o, c: (body(o), c)[1], jnp.int32(0))


def moving_kernel(
    n, ncols, width, cap, group,
    right_ref, left_ref, updates_ref, pattern_ref, targets_ref, pos_ref,
    coded_ref,
    both_ref, req_out, req_in, hot_ref, pick_out, pick_in, gather_ref, sel_ref, selt_ref, masked_ref, masked_t_ref, con_out, con_in, mov_out, mov_in, coded_own,
    s0, r0, s1, r1, s2, r2, s3, r3, s4, r4,
):
    me = lax.axis_index("rows")
    mycol = lax.axis_index("cols")
    rows_loc, lanes = both_ref.shape
    total = targets_ref.shape[1]
    children, block, _ = updates_ref.shape
    tiles = pattern_ref.shape[1]
    tile = block // tiles

    def to_row(o):
        return lax.rem(me + o, n)

    def from_row(o):
        return lax.rem(me - o + n, n)

    barrier = pltpu.get_barrier_semaphore()
    _each(n, lambda o: pl.semaphore_signal(
        barrier, inc=1, device_id={"rows": to_row(o)}, device_id_type=MESH))
    for o in range(1, ncols):
        pl.semaphore_signal(
            barrier, inc=1, device_id={"cols": lax.rem(mycol + o, ncols)}, device_id_type=MESH)

    def copy(out, into, send, recv, o):
        return pltpu.make_async_remote_copy(
            src_ref=out.at[to_row(o)], dst_ref=into.at[me], send_sem=send.at[o],
            recv_sem=recv.at[o], device_id={"rows": to_row(o)}, device_id_type=MESH)

    def arrival(out, into, send, recv, o):
        return pltpu.make_async_remote_copy(
            src_ref=out.at[to_row(o)], dst_ref=into.at[from_row(o)], send_sem=send.at[o],
            recv_sem=recv.at[o], device_id={"rows": to_row(o)}, device_id_type=MESH)

    half = width // 2
    sides = ((right_ref, 0), (left_ref, half))
    slot, local = _positions(targets_ref[...], n, rows_loc, cap)
    digits = jnp.where(
        _iota((16, total), 0) < 8, jnp.bitwise_and(local, 255), jnp.right_shift(local, 8))
    digits = digits.astype(F32).astype(BF16)

    def make_request(d, where):
        part = (_iota((cap, total), 0) + d * cap == slot).astype(F32).astype(BF16)
        sel_ref[pl.ds(pl.multiple_of(d * cap, 16), cap), :] = part
        ask = _dot(digits, part, NT)
        where[d, :, :cap] = (ask[:1] + 256.0 * ask[8:9]).astype(jnp.int32)

    pl.semaphore_wait(barrier, n - 1 + ncols - 1)

    def send_request(o):
        make_request(to_row(o), req_out)
        copy(req_out, req_in, s0, r0, o).start()

    _each(n, send_request, far=True)
    make_request(me, req_in)

    both_ref[...] = functools.reduce(jnp.add, [
        _dot(ref[...],
             (_iota((half, lanes), 1) == _iota((half, lanes), 0) + at).astype(F32).astype(BF16), TN)
        for ref, at in sides]).astype(BF16)
    same = _iota((total, total), 0) == _iota((total, total), 1)
    slot_col = jnp.sum(jnp.where(same, slot.astype(F32), 0.0), axis=1, keepdims=True)
    slot_col = slot_col.astype(jnp.int32)

    def make_selt(d):
        at = _iota((total, cap), 1) + d * cap
        selt_ref[d] = (at == slot_col).astype(F32).astype(BF16)

    make_selt(0)
    _each(n, make_selt)
    for c in range(children):
        for a in range(tiles):
            for b in range(tiles):
                part = updates_ref[c, a * tile : (a + 1) * tile, b * tile : (b + 1) * tile]
                keep = jnp.broadcast_to(pattern_ref[c, a, b], part.shape) != 0
                part = jnp.where(keep, part.astype(F32), 0.0)
                masked_ref[c, a * tile : (a + 1) * tile, b * tile : (b + 1) * tile] = part.astype(BF16)
                masked_t_ref[c, b * tile : (b + 1) * tile, a * tile : (a + 1) * tile] = (
                    jnp.transpose(part).astype(BF16))

    def make_pick(s, where):
        wanted = req_in[s][:, :cap]
        hot = (_iota((rows_loc, cap), 0) == wanted).astype(F32).astype(BF16)
        hot_ref[s] = hot
        where[s] = _pack(_dot(hot, both_ref[...], TN), width).astype(BF16)

    def answer(o):
        arrival(req_out, req_in, s0, r0, n - o).wait_recv()
        make_pick(to_row(o), pick_out)
        copy(pick_out, pick_in, s1, r1, o).start()

    _each(n, answer)
    def fetched(s):
        rows = _unpack(pick_in[s].astype(F32), cap, lanes, width).astype(BF16)
        return _dot(selt_ref[s], rows)

    make_pick(me, pick_in)
    gather_ref[...] = fetched(me)

    def take_rows(o):
        arrival(pick_out, pick_in, s1, r1, o).wait_recv()
        gather_ref[...] += fetched(from_row(o))

    _each(n, take_rows)
    gathered = gather_ref[...].astype(BF16)

    parts = []
    for c in range(children):
        some = gathered[c * block : (c + 1) * block]
        fwd = _dot(masked_ref[c], some)
        trn = _dot(masked_t_ref[c], some)
        parts.append(jnp.where(_iota(fwd.shape, 1) < width // 2, fwd, trn))
    contrib = parts[0] if children == 1 else jnp.concatenate(parts, axis=0)
    code_hi, code_lo = _digits(_encode(contrib, width))

    def make_con(d, where):
        part = sel_ref[pl.ds(pl.multiple_of(d * cap, 16), cap), :]
        moved = _pack(_move_exact(part, code_hi, code_lo), width)
        where[d] = moved.astype(jnp.int32).astype(jnp.int16)

    def send_con(o):
        make_con(to_row(o), con_out)
        copy(con_out, con_in, s2, r2, o).start()

    _each(n, send_con, far=True)
    make_con(me, con_in)

    slot2, place = _positions(pos_ref[...], n, rows_loc, group)
    sel2 = (_iota((n * group, rows_loc), 0) == slot2).astype(F32).astype(BF16)
    diag = _iota((rows_loc, rows_loc), 0) == _iota((rows_loc, rows_loc), 1)
    place_col = jnp.sum(jnp.where(diag, place.astype(F32) + 1.0, 0.0), axis=1, keepdims=True)

    def add_from(s, front):
        code = _unpack(con_in[s].astype(jnp.int32).astype(F32), cap, lanes, width)
        hi, lo = _split2(_decode(code, width))
        hot = hot_ref[s]
        return front + _dot(hot, hi) + _dot(hot, lo)

    front = add_from(me, jnp.zeros((rows_loc, lanes), F32))

    def take(o, front):
        arrival(con_out, con_in, s2, r2, o).wait_recv()
        return add_from(from_row(o), front)

    if n <= 17:
        for o in _order(n):
            front = take(o, front)
    else:
        front = lax.fori_loop(1, n, take, front)

    code = jnp.where(_iota(front.shape, 1) == width + 1, place_col, _encode(front, width))
    moved = _move_exact(sel2, *_digits(code))
    for d in range(n):
        block_d = _pack(moved[d * group : (d + 1) * group], width)
        mov_out[d] = block_d.astype(jnp.int32).astype(jnp.int16)

    def send_moved(o):
        copy(mov_out, mov_in, s3, r3, o).start()

    _each(n, send_moved, far=True)
    mov_in[me] = mov_out[me]
    _each(n, lambda o: arrival(mov_out, mov_in, s3, r3, o).wait_recv())
    got = jnp.concatenate(
        [_unpack(mov_in[d].astype(jnp.int32).astype(F32), group, lanes, width) for d in range(n)],
        axis=0)
    landing = got[:, width + 1 : width + 2].astype(jnp.int32) - 1
    hot2 = (_iota((n * group, rows_loc), 1) == landing).astype(F32).astype(BF16)
    coded = _move_exact(hot2, *_digits(got), TN)
    coded_own[...] = _pack(coded, width).astype(jnp.int32).astype(jnp.int16)

    def col_copy(src, slot, to, i):
        return pltpu.make_async_remote_copy(
            src_ref=src, dst_ref=coded_ref.at[slot], send_sem=s4.at[i], recv_sem=r4.at[i],
            device_id={"cols": to}, device_id_type=MESH)

    if ncols == 4:
        across = lax.rem(mycol + 2, 4)
        beside = mycol + 1 - 2 * lax.rem(mycol, 2)
        corner = lax.rem(beside + 2, 4)
        first = col_copy(coded_own, mycol, across, 0)
        first.start()
        second = col_copy(coded_own, mycol, beside, 1)
        second.start()
        coded_ref[mycol] = coded_own[...]
        col_copy(coded_own, across, across, 0).wait_recv()
        third = col_copy(coded_ref.at[across], across, beside, 2)
        third.start()
        col_copy(coded_own, beside, beside, 1).wait_recv()
        col_copy(coded_own, corner, beside, 2).wait_recv()
        col_sends = (first, second, third)
    else:
        col_sends = tuple(
            col_copy(coded_own, mycol, lax.rem(mycol + o, ncols), o) for o in range(1, ncols))
        for send in col_sends:
            send.start()
        coded_ref[mycol] = coded_own[...]
        for o in range(1, ncols):
            came = lax.rem(mycol - o + ncols, ncols)
            col_copy(coded_own, came, came, o).wait_recv()

    for bufs in ((req_out, req_in, s0, r0), (pick_out, pick_in, s1, r1),
                 (con_out, con_in, s2, r2), (mov_out, mov_in, s3, r3)):
        _each(n, lambda o, bufs=bufs: copy(*bufs, o).wait_send())
    for send in col_sends:
        send.wait_send()


def _small_inverse(p):
    m = len(p)
    if m == 1:
        return [[1.0 / p[0][0]]]
    if m == 2:
        inv = 1.0 / (p[0][0] * p[1][1] - p[0][1] * p[1][0])
        return [[p[1][1] * inv, -p[0][1] * inv], [-p[1][0] * inv, p[0][0] * inv]]
    h = m // 2

    def mul(a, b):
        return [
            [functools.reduce(jnp.add, [a[i][k] * b[k][j] for k in range(len(b))])
             for j in range(len(b[0]))]
            for i in range(len(a))
        ]

    a = [row[:h] for row in p[:h]]
    b = [row[h:] for row in p[:h]]
    c = [row[:h] for row in p[h:]]
    d = [row[h:] for row in p[h:]]
    ai = _small_inverse(a)
    cai = mul(c, ai)
    aib = mul(ai, b)
    caib = mul(cai, b)
    si = _small_inverse([[d[i][j] - caib[i][j] for j in range(h)] for i in range(h)])
    aibsi = mul(aib, si)
    sicai = mul(si, cai)
    corr = mul(aibsi, cai)
    top = [[ai[i][j] + corr[i][j] for j in range(h)] + [-aibsi[i][j] for j in range(h)]
           for i in range(h)]
    low = [[-sicai[i][j] for j in range(h)] + list(si[i]) for i in range(h)]
    return top + low


def _spd_inverse(gram, step):
    order = gram.shape[0]
    tiles = [gram[i : i + 8] for i in range(0, order, 8)]
    lane = _iota((8, order), 1)
    sub = _iota((8, order), 0)
    lane1 = _iota((1, order), 1)
    for k in range(0, order, step):
        at, off = k // 8, k % 8
        cols = [[jnp.broadcast_to(t[:, k + j : k + j + 1], (8, order)) for j in range(step)]
                for t in tiles]
        pivot = [[cols[at][j][off + i : off + i + 1] for j in range(step)] for i in range(step)]
        binv = _small_inverse(pivot)
        rows = [
            jnp.where((lane1 >= k) & (lane1 < k + step), (lane1 == k + i).astype(F32),
                      tiles[at][off + i : off + i + 1])
            for i in range(step)
        ]
        fresh = [functools.reduce(jnp.add, [binv[i][j] * rows[j] for j in range(step)])
                 for i in range(step)]
        inside = (lane >= k) & (lane < k + step)
        for x in range(len(tiles)):
            t = jnp.where(inside, 0.0, tiles[x])
            for j in range(step):
                t = t - cols[x][j] * fresh[j]
            if x == at:
                for i in range(step):
                    t = jnp.where(sub == off + i, fresh[i], t)
            tiles[x] = t
    return jnp.concatenate(tiles, axis=0)


def _dot3(a, b, dims):
    ah, al = _split2(a)
    bh, bl = _split2(b)
    return _dot(ah, bh, dims) + (_dot(ah, bl, dims) + _dot(al, bh, dims))


LIMIT = 64.0
SETTLED = 1e-5


def _solve_limits():
    limits = []
    for steps in range(4, 9):
        low, high = 1.0, 1e6
        for _ in range(100):
            mid = (low * high) ** 0.5
            rho = (mid - 1.0) / (mid + 1.0)
            for _ in range(steps):
                rho = rho * rho / (2.0 - rho * rho)
            low, high = (mid, high) if rho <= SETTLED else (low, mid)
        limits.append(low)
        if low >= LIMIT:
            break
    return limits


def _left(a):
    return jnp.concatenate(_split2(a), axis=1)


def _right(b):
    both = jnp.concatenate(_split2(b), axis=1)
    return jnp.concatenate([both, both], axis=0)


def _product(left, right):
    both = _dot(left, right)
    half = both.shape[1] // 2
    return both[:, :half] + both[:, half:]


def _narrow(rho):
    scale = 1.0 / (2.0 - rho * rho)
    return 2.0 * scale, rho * rho * scale


def _settling_solve(cross, gram, top):
    order = gram.shape[0]
    bound = jnp.max(top)
    eye = (_iota((order, order), 0) == _iota((order, order), 1)).astype(F32)
    limits = _solve_limits()
    count = 2 + functools.reduce(
        jnp.add, [(bound > limit).astype(jnp.int32) for limit in limits[:-1]])
    inv = 1.0 / (top + 1.0)
    scale, rho = _narrow((top - 1.0) * inv)
    first = 2.0 * inv
    x = (first * scale) * (2.0 * eye - first * gram)
    gram_left = _left(gram)

    def step(_, carry):
        x, rho = carry
        scale, rho = _narrow(rho)
        rest = scale * (2.0 * eye - _product(gram_left, _right(x)))
        return _product(_left(x), _right(rest)), rho

    x, rho = lax.fori_loop(0, count, step, (x, rho))
    right = _right(x)
    scale, rho = _narrow(rho)
    rest = scale * (2.0 * eye - _product(gram_left, right))
    return _product(_left(_product(_left(cross), right)), _right(rest))


def leaf_kernel(width, coded_ref, pivots_ref, fwd_ref, trn_ref, interp_ref, hi_ref, lo_ref):
    ncols = coded_ref.shape[0]
    rows_loc = interp_ref.shape[0]
    lanes = hi_ref.shape[1] // ncols
    half = width // 2

    def values(c):
        code = coded_ref[c].astype(jnp.int32).astype(F32)
        return _decode(_unpack(code, rows_loc, lanes, width), width)

    mycol = lax.axis_index("cols")
    own = jnp.transpose(values(mycol))
    fwd_ref[...] = own[:half]
    trn_ref[...] = own[half:width]
    for c in range(ncols):
        hi, lo = _split2(values(c))
        hi_ref[:, c * lanes : (c + 1) * lanes] = hi
        lo_ref[:, c * lanes : (c + 1) * lanes] = lo
    for leaf in range(rows_loc // LEAF):
        at = slice(leaf * LEAF, (leaf + 1) * LEAF)
        hi, lo = hi_ref[at, :], lo_ref[at, :]
        pick = (_iota((LEAF, RANK), 0) == pivots_ref[leaf : leaf + 1, :]).astype(F32).astype(BF16)
        shi = _dot(pick, hi, TN).astype(BF16)
        slo = _dot(pick, lo, TN).astype(BF16)
        gram = _dot(shi, shi, NT) + (_dot(shi, slo, NT) + _dot(slo, shi, NT))
        eye = (_iota((RANK, RANK), 0) == _iota((RANK, RANK), 1)).astype(F32)
        gram = gram * (1.0 / (2.0 * K)) + eye
        cross = _dot(hi, shi, NT) + (_dot(hi, slo, NT) + _dot(lo, shi, NT))
        cross = cross * (1.0 / (2.0 * K))
        top = jnp.max(jnp.sum(jnp.abs(gram), axis=0, keepdims=True), axis=1, keepdims=True)
        settles = jnp.max(top) <= LIMIT

        @pl.when(settles)
        def _():
            interp_ref[at, :] = _settling_solve(cross, gram, top)

        @pl.when(jnp.logical_not(settles))
        def _():
            interp_ref[at, :] = _dot3(cross, _spd_inverse(gram, STEP), ((1,), (0,)))


def per_device(n, ncols, right_sample, left_sample, updates, pattern, targets, cluster_pos, pivots):
    children, block, _ = updates.shape
    rows_loc, half = right_sample.shape
    width = 2 * half
    lanes = _up(width + 2, 128)
    cap = _up(max(2, 3 * children * block // (2 * n)), 16)
    group = _up(rows_loc // n, 16)
    vmem = pl.BlockSpec(memory_space=pltpu.VMEM)
    smem = pl.BlockSpec(memory_space=pltpu.SMEM)
    i16 = jnp.int16
    coded = pl.pallas_call(
        functools.partial(moving_kernel, n, ncols, width, cap, group),
        out_shape=jax.ShapeDtypeStruct((ncols, _packed(rows_loc, lanes, width), 128), i16),
        in_specs=[vmem, vmem, vmem, smem, vmem, vmem],
        out_specs=vmem,
        scratch_shapes=[
            pltpu.VMEM((rows_loc, lanes), BF16),
            pltpu.VMEM((n, 1, _up(cap, 128)), jnp.int32),
            pltpu.VMEM((n, 1, _up(cap, 128)), jnp.int32),
            pltpu.VMEM((n, rows_loc, cap), BF16),
            pltpu.VMEM((n, _packed(cap, lanes, width), 128), BF16),
            pltpu.VMEM((n, _packed(cap, lanes, width), 128), BF16),
            pltpu.VMEM((children * block, lanes), F32),
            pltpu.VMEM((n * cap, children * block), BF16),
            pltpu.VMEM((n, children * block, cap), BF16),
            pltpu.VMEM(updates.shape, BF16),
            pltpu.VMEM(updates.shape, BF16),
            pltpu.VMEM((n, _packed(cap, lanes, width), 128), i16),
            pltpu.VMEM((n, _packed(cap, lanes, width), 128), i16),
            pltpu.VMEM((n, _packed(group, lanes, width), 128), i16),
            pltpu.VMEM((n, _packed(group, lanes, width), 128), i16),
            pltpu.VMEM((_packed(rows_loc, lanes, width), 128), i16),
        ]
        + [pltpu.SemaphoreType.DMA((n,))] * 8
        + [pltpu.SemaphoreType.DMA((ncols,))] * 2,
        compiler_params=pltpu.CompilerParams(collective_id=0, has_side_effects=True),
        name="moving",
    )(right_sample.T, left_sample.T, updates, pattern, targets.reshape(1, -1), cluster_pos.reshape(1, -1))
    forward, transposed, interp = pl.pallas_call(
        functools.partial(leaf_kernel, width),
        out_shape=(
            jax.ShapeDtypeStruct((half, rows_loc), F32),
            jax.ShapeDtypeStruct((half, rows_loc), F32),
            jax.ShapeDtypeStruct((rows_loc, RANK), F32),
        ),
        in_specs=[vmem, vmem],
        out_specs=(vmem, vmem, vmem),
        scratch_shapes=[pltpu.VMEM((rows_loc, ncols * lanes), BF16)] * 2,
        name="leaf",
    )(coded, pivots)
    return forward.T, transposed.T, interp


def solution(mesh):
    sizes = dict(mesh.shape)
    return jax.shard_map(
        functools.partial(per_device, sizes["rows"], sizes["cols"]),
        mesh=mesh,
        in_specs=(
            P("rows", "cols"),
            P("rows", "cols"),
            P("rows", None, None),
            P("rows", None, None),
            P("rows", None),
            P("rows"),
            P("rows", None),
        ),
        out_specs=(P("rows", "cols"), P("rows", "cols"), P("rows", None)),
        check_vma=False,
    )
```

```python
import functools

import jax
import jax.numpy as jnp
from jax import lax
from jax.experimental import pallas as pl
from jax.experimental.pallas import tpu as pltpu
from jax.sharding import PartitionSpec as P

K = 320
LEAF = 256
RANK = 128
MESH = pl.DeviceIdType.MESH
F32 = jnp.float32
BF16 = jnp.bfloat16
QMAX = 32766.0
STEP = 4


def _up(value, unit):
    return -(-value // unit) * unit


def _dot(a, b, dims=((1,), (0,))):
    return lax.dot_general(a, b, (dims, ((), ())), preferred_element_type=F32)


TN = ((0,), (0,))
NT = ((1,), (1,))


def _iota(shape, dim):
    return lax.broadcasted_iota(jnp.int32, shape, dim)


def _split2(x):
    hi = x.astype(BF16)
    return hi, (x - hi.astype(F32)).astype(BF16)


def _digits(q):
    hi = jnp.floor(q * (1.0 / 256.0))
    return hi.astype(BF16), (q - 256.0 * hi).astype(BF16)


def _move_exact(sel, hi, lo, dims=((1,), (0,))):
    return 256.0 * _dot(sel, hi, dims) + _dot(sel, lo, dims)


def _encode(x, width):
    lane = _iota(x.shape, 1)
    top = jnp.max(jnp.where(lane < width, jnp.abs(x), 0.0), axis=1, keepdims=True)
    expo = jnp.clip(
        jnp.ceil(jnp.log(jnp.maximum(top, 1e-30)) * 1.4426950408889634 + 0.001), -96.0, 120.0
    )
    code = jnp.floor(x * (QMAX / jnp.exp2(expo)) + 0.5)
    return jnp.where(lane < width, code, jnp.where(lane == width, expo, 0.0))


def _decode(q, width):
    lane = _iota(q.shape, 1)
    scale = jnp.exp2(q[:, width : width + 1]) * (1.0 / QMAX)
    return jnp.where(lane < width, q * scale, 0.0)


def _code_rows(x):
    top = jnp.max(jnp.abs(x), axis=0, keepdims=True)
    expo = jnp.clip(
        jnp.ceil(jnp.log(jnp.maximum(top, 1e-30)) * 1.4426950408889634 + 0.001), -96.0, 120.0
    )
    return expo, jnp.floor(x * (QMAX / jnp.exp2(expo)) + 0.5)


def _encode_part(part, pickt):
    on = pickt.astype(F32) > 0.5
    expo, code = _code_rows(jnp.where(on, 0.0, part))
    own_expo, own_code = _code_rows(jnp.sum(jnp.where(on, part, 0.0), axis=0, keepdims=True))
    row = _iota((16, part.shape[1]), 0)
    tail = jnp.where(row == 0, expo, jnp.where(row == 1, own_expo, jnp.where(row == 2, own_code, 0.0)))
    return jnp.concatenate([code, tail], axis=0).astype(jnp.int32).astype(jnp.int16)


def _folds(rows, lanes, width):
    stride = width + 2 - (lanes - 128)
    return max(f for f in range(1, 9)
               if f == 1 or (rows % f == 0 and (rows // f) % 16 == 0 and f * stride <= 128))


def _packed(rows, lanes, width):
    return rows * (lanes // 128 - 1) + rows // _folds(rows, lanes, width)


def _pack(x, width):
    rows, lanes = x.shape
    folds = _folds(rows, lanes, width)
    stride = width + 2 - (lanes - 128)
    part = rows // folds
    last = x[:, lanes - 128 :]
    tail = last[:part]
    for g in range(1, folds):
        tail = tail + pltpu.roll(last[g * part : (g + 1) * part], g * stride, axis=1)
    return jnp.concatenate([x[:, i : i + 128] for i in range(0, lanes - 128, 128)] + [tail], axis=0)


def _unpack(y, rows, lanes, width):
    folds = _folds(rows, lanes, width)
    stride = width + 2 - (lanes - 128)
    panels = lanes // 128 - 1
    tail = y[panels * rows :]
    pieces = [tail] + [pltpu.roll(tail, 128 - g * stride, axis=1) for g in range(1, folds)]
    last = jnp.concatenate(pieces, axis=0) if folds > 1 else tail
    last = jnp.where(_iota(last.shape, 1) < stride, last, 0.0)
    return jnp.concatenate([y[i * rows : (i + 1) * rows] for i in range(panels)] + [last], axis=1)


def _positions(row, count, span, stride):
    length = row.shape[1]
    rows8 = _up(count, 16)
    holder = _iota((rows8, length), 0)
    hot = (row >= holder * span) & (row < (holder + 1) * span)
    hot_f = hot.astype(F32)
    before = (_iota((length, length), 0) < _iota((length, length), 1)).astype(F32).astype(BF16)
    rank = _dot(hot_f.astype(BF16), before)
    slot = jnp.sum(hot_f * (rank + (holder * stride).astype(F32)), axis=0, keepdims=True)
    base = jnp.sum(hot_f * (holder * span).astype(F32), axis=0, keepdims=True)
    return slot.astype(jnp.int32), row - base.astype(jnp.int32)


def _order(count):
    return sorted(range(1, count), key=lambda o: (min(o, count - o), o))


def _each(count, body, far=False):
    if count <= 17:
        for o in _order(count)[:: -1 if far else 1]:
            body(o)
    else:
        lax.fori_loop(1, count, lambda o, c: (body(o), c)[1], jnp.int32(0))


def moving_kernel(
    n, ncols, width, cap, group,
    right_ref, left_ref, updates_ref, pattern_ref, targets_ref, pos_ref, pivots_ref,
    parts_ref, own_ref, pickt_ref,
    both_ref, req_out, req_in, hot_ref, pick_out, pick_in, gather_ref, sel_ref, selt_ref, masked_ref, masked_t_ref, con_out, con_in, mov_out, mov_in, part_own,
    s0, r0, s1, r1, s2, r2, s3, r3, s4, r4,
):
    me = lax.axis_index("rows")
    mycol = lax.axis_index("cols")
    rows_loc, lanes = both_ref.shape
    total = targets_ref.shape[1]
    children, block, _ = updates_ref.shape
    tiles = pattern_ref.shape[1]
    tile = block // tiles

    def to_row(o):
        return lax.rem(me + o, n)

    def from_row(o):
        return lax.rem(me - o + n, n)

    barrier = pltpu.get_barrier_semaphore()
    _each(n, lambda o: pl.semaphore_signal(
        barrier, inc=1, device_id={"rows": to_row(o)}, device_id_type=MESH))
    for o in range(1, ncols):
        pl.semaphore_signal(
            barrier, inc=1, device_id={"cols": lax.rem(mycol + o, ncols)}, device_id_type=MESH)

    def copy(out, into, send, recv, o):
        return pltpu.make_async_remote_copy(
            src_ref=out.at[to_row(o)], dst_ref=into.at[me], send_sem=send.at[o],
            recv_sem=recv.at[o], device_id={"rows": to_row(o)}, device_id_type=MESH)

    def arrival(out, into, send, recv, o):
        return pltpu.make_async_remote_copy(
            src_ref=out.at[to_row(o)], dst_ref=into.at[from_row(o)], send_sem=send.at[o],
            recv_sem=recv.at[o], device_id={"rows": to_row(o)}, device_id_type=MESH)

    half = width // 2
    sides = ((right_ref, 0), (left_ref, half))
    slot, local = _positions(targets_ref[...], n, rows_loc, cap)
    digits = jnp.where(
        _iota((16, total), 0) < 8, jnp.bitwise_and(local, 255), jnp.right_shift(local, 8))
    digits = digits.astype(F32).astype(BF16)

    def make_request(d, where):
        part = (_iota((cap, total), 0) + d * cap == slot).astype(F32).astype(BF16)
        sel_ref[pl.ds(pl.multiple_of(d * cap, 16), cap), :] = part
        ask = _dot(digits, part, NT)
        where[d, :, :cap] = (ask[:1] + 256.0 * ask[8:9]).astype(jnp.int32)

    _each(n, lambda o: make_request(to_row(o), req_out), far=True)
    pl.semaphore_wait(barrier, n - 1 + ncols - 1)
    _each(n, lambda o: copy(req_out, req_in, s0, r0, o).start(), far=True)
    make_request(me, req_in)
    chosen = _iota((rows_loc, RANK), 0) == pivots_ref[...]
    pickt_ref[...] = jnp.transpose(chosen.astype(F32)).astype(BF16)

    both_ref[...] = functools.reduce(jnp.add, [
        _dot(ref[...],
             (_iota((half, lanes), 1) == _iota((half, lanes), 0) + at).astype(F32).astype(BF16), TN)
        for ref, at in sides]).astype(BF16)
    same = _iota((total, total), 0) == _iota((total, total), 1)
    slot_col = jnp.sum(jnp.where(same, slot.astype(F32), 0.0), axis=1, keepdims=True)
    slot_col = slot_col.astype(jnp.int32)

    def make_selt(d):
        at = _iota((total, cap), 1) + d * cap
        selt_ref[d] = (at == slot_col).astype(F32).astype(BF16)

    make_selt(0)
    _each(n, make_selt)
    for c in range(children):
        for a in range(tiles):
            for b in range(tiles):
                part = updates_ref[c, a * tile : (a + 1) * tile, b * tile : (b + 1) * tile]
                keep = jnp.broadcast_to(pattern_ref[c, a, b], part.shape) != 0
                part = jnp.where(keep, part.astype(F32), 0.0)
                masked_ref[c, a * tile : (a + 1) * tile, b * tile : (b + 1) * tile] = part.astype(BF16)
                masked_t_ref[c, b * tile : (b + 1) * tile, a * tile : (a + 1) * tile] = (
                    jnp.transpose(part).astype(BF16))

    def make_pick(s, where):
        wanted = req_in[s][:, :cap]
        hot = (_iota((rows_loc, cap), 0) == wanted).astype(F32).astype(BF16)
        hot_ref[s] = hot
        where[s] = _pack(_dot(hot, both_ref[...], TN), width).astype(BF16)

    def answer(o):
        arrival(req_out, req_in, s0, r0, n - o).wait_recv()
        make_pick(to_row(o), pick_out)
        copy(pick_out, pick_in, s1, r1, o).start()

    _each(n, answer)
    def fetched(s):
        rows = _unpack(pick_in[s].astype(F32), cap, lanes, width).astype(BF16)
        return _dot(selt_ref[s], rows)

    make_pick(me, pick_in)
    gather_ref[...] = fetched(me)

    def take_rows(o):
        arrival(pick_out, pick_in, s1, r1, o).wait_recv()
        gather_ref[...] += fetched(from_row(o))

    _each(n, take_rows)
    gathered = gather_ref[...].astype(BF16)

    parts = []
    for c in range(children):
        some = gathered[c * block : (c + 1) * block]
        fwd = _dot(masked_ref[c], some)
        trn = _dot(masked_t_ref[c], some)
        parts.append(jnp.where(_iota(fwd.shape, 1) < width // 2, fwd, trn))
    contrib = parts[0] if children == 1 else jnp.concatenate(parts, axis=0)
    code_hi, code_lo = _digits(_encode(contrib, width))

    def make_con(d, where):
        part = sel_ref[pl.ds(pl.multiple_of(d * cap, 16), cap), :]
        moved = _pack(_move_exact(part, code_hi, code_lo), width)
        where[d] = moved.astype(jnp.int32).astype(jnp.int16)

    def send_con(o):
        make_con(to_row(o), con_out)
        copy(con_out, con_in, s2, r2, o).start()

    _each(n, send_con, far=True)
    make_con(me, con_in)

    slot2, place = _positions(pos_ref[...], n, rows_loc, group)
    sel2 = (_iota((n * group, rows_loc), 0) == slot2).astype(F32).astype(BF16)
    diag = _iota((rows_loc, rows_loc), 0) == _iota((rows_loc, rows_loc), 1)
    place_col = jnp.sum(jnp.where(diag, place.astype(F32) + 1.0, 0.0), axis=1, keepdims=True)

    def add_from(s, front):
        code = _unpack(con_in[s].astype(jnp.int32).astype(F32), cap, lanes, width)
        hi, lo = _split2(_decode(code, width))
        hot = hot_ref[s]
        return front + _dot(hot, hi) + _dot(hot, lo)

    front = add_from(me, jnp.zeros((rows_loc, lanes), F32))

    def take(o, front):
        arrival(con_out, con_in, s2, r2, o).wait_recv()
        return add_from(from_row(o), front)

    if n <= 17:
        for o in _order(n):
            front = take(o, front)
    else:
        front = lax.fori_loop(1, n, take, front)

    code = jnp.where(_iota(front.shape, 1) == width + 1, place_col, _encode(front, width))
    moved = _move_exact(sel2, *_digits(code))
    for d in range(n):
        block_d = _pack(moved[d * group : (d + 1) * group], width)
        mov_out[d] = block_d.astype(jnp.int32).astype(jnp.int16)

    def send_moved(o):
        copy(mov_out, mov_in, s3, r3, o).start()

    _each(n, send_moved, far=True)
    mov_in[me] = mov_out[me]
    _each(n, lambda o: arrival(mov_out, mov_in, s3, r3, o).wait_recv())
    got = jnp.concatenate(
        [_unpack(mov_in[d].astype(jnp.int32).astype(F32), group, lanes, width) for d in range(n)],
        axis=0)
    landing = got[:, width + 1 : width + 2].astype(jnp.int32) - 1
    hot2 = (_iota((n * group, rows_loc), 1) == landing).astype(F32).astype(BF16)
    coded = _move_exact(hot2, *_digits(got), TN)
    values = _decode(coded, width)
    hi, lo = _split2(values)
    pickt = pickt_ref[...]
    shi = _dot(pickt, hi).astype(BF16)
    slo = _dot(pickt, lo).astype(BF16)
    part = _dot(shi, hi, NT) + (_dot(shi, lo, NT) + _dot(slo, hi, NT))
    part_own[...] = _encode_part(part * (1.0 / (2.0 * K)), pickt)

    def col_copy(src, slot, to, i):
        return pltpu.make_async_remote_copy(
            src_ref=src, dst_ref=parts_ref.at[slot], send_sem=s4.at[i], recv_sem=r4.at[i],
            device_id={"cols": to}, device_id_type=MESH)

    if ncols == 4:
        across = lax.rem(mycol + 2, 4)
        beside = mycol + 1 - 2 * lax.rem(mycol, 2)
        corner = lax.rem(beside + 2, 4)
        first = col_copy(part_own, mycol, across, 0)
        first.start()
        second = col_copy(part_own, mycol, beside, 1)
        second.start()
        parts_ref[mycol] = part_own[...]
        own_ref[...] = jnp.transpose(values)[:width]
        col_copy(part_own, across, across, 0).wait_recv()
        third = col_copy(parts_ref.at[across], across, beside, 2)
        third.start()
        col_copy(part_own, beside, beside, 1).wait_recv()
        col_copy(part_own, corner, beside, 2).wait_recv()
        col_sends = (first, second, third)
    else:
        col_sends = tuple(
            col_copy(part_own, mycol, lax.rem(mycol + o, ncols), o) for o in range(1, ncols))
        for send in col_sends:
            send.start()
        parts_ref[mycol] = part_own[...]
        own_ref[...] = jnp.transpose(values)[:width]
        for o in range(1, ncols):
            came = lax.rem(mycol - o + ncols, ncols)
            col_copy(part_own, came, came, o).wait_recv()

    for bufs in ((req_out, req_in, s0, r0), (pick_out, pick_in, s1, r1),
                 (con_out, con_in, s2, r2), (mov_out, mov_in, s3, r3)):
        _each(n, lambda o, bufs=bufs: copy(*bufs, o).wait_send())
    for send in col_sends:
        send.wait_send()


def _small_inverse(p):
    m = len(p)
    if m == 1:
        return [[1.0 / p[0][0]]]
    if m == 2:
        inv = 1.0 / (p[0][0] * p[1][1] - p[0][1] * p[1][0])
        return [[p[1][1] * inv, -p[0][1] * inv], [-p[1][0] * inv, p[0][0] * inv]]
    h = m // 2

    def mul(a, b):
        return [
            [functools.reduce(jnp.add, [a[i][k] * b[k][j] for k in range(len(b))])
             for j in range(len(b[0]))]
            for i in range(len(a))
        ]

    a = [row[:h] for row in p[:h]]
    b = [row[h:] for row in p[:h]]
    c = [row[:h] for row in p[h:]]
    d = [row[h:] for row in p[h:]]
    ai = _small_inverse(a)
    cai = mul(c, ai)
    aib = mul(ai, b)
    caib = mul(cai, b)
    si = _small_inverse([[d[i][j] - caib[i][j] for j in range(h)] for i in range(h)])
    aibsi = mul(aib, si)
    sicai = mul(si, cai)
    corr = mul(aibsi, cai)
    top = [[ai[i][j] + corr[i][j] for j in range(h)] + [-aibsi[i][j] for j in range(h)]
           for i in range(h)]
    low = [[-sicai[i][j] for j in range(h)] + list(si[i]) for i in range(h)]
    return top + low


def _spd_inverse(gram, step):
    order = gram.shape[0]
    tiles = [gram[i : i + 8] for i in range(0, order, 8)]
    lane = _iota((8, order), 1)
    sub = _iota((8, order), 0)
    lane1 = _iota((1, order), 1)
    for k in range(0, order, step):
        at, off = k // 8, k % 8
        cols = [[jnp.broadcast_to(t[:, k + j : k + j + 1], (8, order)) for j in range(step)]
                for t in tiles]
        pivot = [[cols[at][j][off + i : off + i + 1] for j in range(step)] for i in range(step)]
        binv = _small_inverse(pivot)
        rows = [
            jnp.where((lane1 >= k) & (lane1 < k + step), (lane1 == k + i).astype(F32),
                      tiles[at][off + i : off + i + 1])
            for i in range(step)
        ]
        fresh = [functools.reduce(jnp.add, [binv[i][j] * rows[j] for j in range(step)])
                 for i in range(step)]
        inside = (lane >= k) & (lane < k + step)
        for x in range(len(tiles)):
            t = jnp.where(inside, 0.0, tiles[x])
            for j in range(step):
                t = t - cols[x][j] * fresh[j]
            if x == at:
                for i in range(step):
                    t = jnp.where(sub == off + i, fresh[i], t)
            tiles[x] = t
    return jnp.concatenate(tiles, axis=0)


def _dot3(a, b, dims):
    ah, al = _split2(a)
    bh, bl = _split2(b)
    return _dot(ah, bh, dims) + (_dot(ah, bl, dims) + _dot(al, bh, dims))


LIMIT = 64.0
SETTLED = 1e-5


def _solve_limits():
    limits = []
    for steps in range(4, 9):
        low, high = 1.0, 1e6
        for _ in range(100):
            mid = (low * high) ** 0.5
            rho = (mid - 1.0) / (mid + 1.0)
            for _ in range(steps):
                rho = rho * rho / (2.0 - rho * rho)
            low, high = (mid, high) if rho <= SETTLED else (low, mid)
        limits.append(low)
        if low >= LIMIT:
            break
    return limits


def _left(a):
    return jnp.concatenate(_split2(a), axis=1)


def _right(b):
    both = jnp.concatenate(_split2(b), axis=1)
    return jnp.concatenate([both, both], axis=0)


def _product(left, right):
    both = _dot(left, right)
    half = both.shape[1] // 2
    return both[:, :half] + both[:, half:]


def _narrow(rho):
    scale = 1.0 / (2.0 - rho * rho)
    return 2.0 * scale, rho * rho * scale


def _settling_solve(cross, gram, top):
    order = gram.shape[0]
    bound = jnp.max(top)
    eye = (_iota((order, order), 0) == _iota((order, order), 1)).astype(F32)
    limits = _solve_limits()
    count = 2 + functools.reduce(
        jnp.add, [(bound > limit).astype(jnp.int32) for limit in limits[:-1]])
    inv = 1.0 / (top + 1.0)
    scale, rho = _narrow((top - 1.0) * inv)
    first = 2.0 * inv
    x = (first * scale) * (2.0 * eye - first * gram)
    gram_left = _left(gram)

    def step(_, carry):
        x, rho = carry
        scale, rho = _narrow(rho)
        rest = scale * (2.0 * eye - _product(gram_left, _right(x)))
        return _product(_left(x), _right(rest)), rho

    cross_left = _left(jnp.transpose(cross))
    for _ in range(2):
        x, rho = step(0, (x, rho))
    x, rho = lax.fori_loop(2, count, step, (x, rho))
    right = _right(x)
    scale, rho = _narrow(rho)
    rest = scale * (2.0 * eye - _product(gram_left, right))
    return _product(_left(_product(cross_left, right)), _right(rest))


def leaf_kernel(parts_ref, own_ref, pickt_ref, pivots_ref, fwd_ref, trn_ref, interp_ref):
    ncols = parts_ref.shape[0]
    half = fwd_ref.shape[0]
    fwd_ref[...] = own_ref[:half]
    trn_ref[...] = own_ref[half:]
    cross, diag = 0.0, 0.0
    for c in range(ncols):
        code = parts_ref[c].astype(jnp.int32).astype(F32)
        tail = code[RANK:]
        cross = cross + code[:RANK] * (jnp.exp2(tail[:1]) * (1.0 / QMAX))
        diag = diag + tail[2:3] * (jnp.exp2(tail[1:2]) * (1.0 / QMAX))
    cross = cross + pickt_ref[...].astype(F32) * diag
    pick = (_iota((LEAF, RANK), 0) == pivots_ref[...]).astype(F32).astype(BF16)
    eye = (_iota((RANK, RANK), 0) == _iota((RANK, RANK), 1)).astype(F32)
    hi, lo = _split2(cross)
    gram = _dot(hi, pick) + _dot(lo, pick) + eye
    top = jnp.max(jnp.sum(jnp.abs(gram), axis=1, keepdims=True), axis=0, keepdims=True)
    settles = jnp.max(top) <= LIMIT

    @pl.when(settles)
    def _():
        interp_ref[...] = _settling_solve(cross, gram, top)

    @pl.when(jnp.logical_not(settles))
    def _():
        interp_ref[...] = _dot3(jnp.transpose(cross), _spd_inverse(gram, STEP), ((1,), (0,)))


def per_device(n, ncols, right_sample, left_sample, updates, pattern, targets, cluster_pos, pivots):
    children, block, _ = updates.shape
    rows_loc, half = right_sample.shape
    width = 2 * half
    lanes = _up(width + 2, 128)
    cap = _up(max(2, 3 * children * block // (2 * n)), 16)
    group = _up(rows_loc // n, 16)
    vmem = pl.BlockSpec(memory_space=pltpu.VMEM)
    smem = pl.BlockSpec(memory_space=pltpu.SMEM)
    i16 = jnp.int16
    parts, own, pickt = pl.pallas_call(
        functools.partial(moving_kernel, n, ncols, width, cap, group),
        out_shape=(
            jax.ShapeDtypeStruct((ncols, RANK + 16, LEAF), i16),
            jax.ShapeDtypeStruct((width, rows_loc), F32),
            jax.ShapeDtypeStruct((RANK, LEAF), BF16),
        ),
        in_specs=[vmem, vmem, vmem, smem, vmem, vmem, vmem],
        out_specs=(vmem, vmem, vmem),
        scratch_shapes=[
            pltpu.VMEM((rows_loc, lanes), BF16),
            pltpu.VMEM((n, 1, _up(cap, 128)), jnp.int32),
            pltpu.VMEM((n, 1, _up(cap, 128)), jnp.int32),
            pltpu.VMEM((n, rows_loc, cap), BF16),
            pltpu.VMEM((n, _packed(cap, lanes, width), 128), BF16),
            pltpu.VMEM((n, _packed(cap, lanes, width), 128), BF16),
            pltpu.VMEM((children * block, lanes), F32),
            pltpu.VMEM((n * cap, children * block), BF16),
            pltpu.VMEM((n, children * block, cap), BF16),
            pltpu.VMEM(updates.shape, BF16),
            pltpu.VMEM(updates.shape, BF16),
            pltpu.VMEM((n, _packed(cap, lanes, width), 128), i16),
            pltpu.VMEM((n, _packed(cap, lanes, width), 128), i16),
            pltpu.VMEM((n, _packed(group, lanes, width), 128), i16),
            pltpu.VMEM((n, _packed(group, lanes, width), 128), i16),
            pltpu.VMEM((RANK + 16, LEAF), i16),
        ]
        + [pltpu.SemaphoreType.DMA((n,))] * 8
        + [pltpu.SemaphoreType.DMA((ncols,))] * 2,
        compiler_params=pltpu.CompilerParams(collective_id=0, has_side_effects=True),
        name="moving",
    )(right_sample.T, left_sample.T, updates, pattern, targets.reshape(1, -1), cluster_pos.reshape(1, -1), pivots)
    forward, transposed, interp = pl.pallas_call(
        leaf_kernel,
        out_shape=(
            jax.ShapeDtypeStruct((half, rows_loc), F32),
            jax.ShapeDtypeStruct((half, rows_loc), F32),
            jax.ShapeDtypeStruct((rows_loc, RANK), F32),
        ),
        in_specs=[vmem] * 4,
        out_specs=(vmem, vmem, vmem),
        name="leaf",
    )(parts, own, pickt, pivots)
    return forward.T, transposed.T, interp


def solution(mesh):
    sizes = dict(mesh.shape)
    return jax.shard_map(
        functools.partial(per_device, sizes["rows"], sizes["cols"]),
        mesh=mesh,
        in_specs=(
            P("rows", "cols"),
            P("rows", "cols"),
            P("rows", None, None),
            P("rows", None, None),
            P("rows", None),
            P("rows"),
            P("rows", None),
        ),
        out_specs=(P("rows", "cols"), P("rows", "cols"), P("rows", None)),
        check_vma=False,
    )
```

```python
import functools

import jax
import jax.numpy as jnp
from jax import lax
from jax.experimental import pallas as pl
from jax.experimental.pallas import tpu as pltpu
from jax.sharding import PartitionSpec as P

K = 320
LEAF = 256
RANK = 128
MESH = pl.DeviceIdType.MESH
F32 = jnp.float32
BF16 = jnp.bfloat16
QMAX = 32766.0
STEP = 4


def _up(value, unit):
    return -(-value // unit) * unit


def _dot(a, b, dims=((1,), (0,))):
    return lax.dot_general(a, b, (dims, ((), ())), preferred_element_type=F32)


TN = ((0,), (0,))
NT = ((1,), (1,))


def _iota(shape, dim):
    return lax.broadcasted_iota(jnp.int32, shape, dim)


def _split2(x):
    hi = x.astype(BF16)
    return hi, (x - hi.astype(F32)).astype(BF16)


def _digits(q):
    hi = jnp.floor(q * (1.0 / 256.0))
    return hi.astype(BF16), (q - 256.0 * hi).astype(BF16)


def _move_exact(sel, hi, lo, dims=((1,), (0,))):
    return 256.0 * _dot(sel, hi, dims) + _dot(sel, lo, dims)


def _encode(x, width):
    lane = _iota(x.shape, 1)
    top = jnp.max(jnp.where(lane < width, jnp.abs(x), 0.0), axis=1, keepdims=True)
    expo = jnp.clip(
        jnp.ceil(jnp.log(jnp.maximum(top, 1e-30)) * 1.4426950408889634 + 0.001), -96.0, 120.0
    )
    code = jnp.floor(x * (QMAX / jnp.exp2(expo)) + 0.5)
    return jnp.where(lane < width, code, jnp.where(lane == width, expo, 0.0))


def _decode(q, width):
    lane = _iota(q.shape, 1)
    scale = jnp.exp2(q[:, width : width + 1]) * (1.0 / QMAX)
    return jnp.where(lane < width, q * scale, 0.0)


def _code_rows(x):
    top = jnp.max(jnp.abs(x), axis=0, keepdims=True)
    expo = jnp.clip(
        jnp.ceil(jnp.log(jnp.maximum(top, 1e-30)) * 1.4426950408889634 + 0.001), -96.0, 120.0
    )
    return expo, jnp.floor(x * (QMAX / jnp.exp2(expo)) + 0.5)


def _encode_part(part, pickt):
    on = pickt.astype(F32) > 0.5
    expo, code = _code_rows(jnp.where(on, 0.0, part))
    own_expo, own_code = _code_rows(jnp.sum(jnp.where(on, part, 0.0), axis=0, keepdims=True))
    row = _iota((16, part.shape[1]), 0)
    tail = jnp.where(row == 0, expo, jnp.where(row == 1, own_expo, jnp.where(row == 2, own_code, 0.0)))
    return jnp.concatenate([code, tail], axis=0).astype(jnp.int32).astype(jnp.int16)


def _folds(rows, lanes, width):
    stride = width + 2 - (lanes - 128)
    return max(f for f in range(1, 9)
               if f == 1 or (rows % f == 0 and (rows // f) % 16 == 0 and f * stride <= 128))


def _packed(rows, lanes, width):
    return rows * (lanes // 128 - 1) + rows // _folds(rows, lanes, width)


def _pack(x, width):
    rows, lanes = x.shape
    folds = _folds(rows, lanes, width)
    stride = width + 2 - (lanes - 128)
    part = rows // folds
    last = x[:, lanes - 128 :]
    tail = last[:part]
    for g in range(1, folds):
        tail = tail + pltpu.roll(last[g * part : (g + 1) * part], g * stride, axis=1)
    return jnp.concatenate([x[:, i : i + 128] for i in range(0, lanes - 128, 128)] + [tail], axis=0)


def _unpack(y, rows, lanes, width):
    folds = _folds(rows, lanes, width)
    stride = width + 2 - (lanes - 128)
    panels = lanes // 128 - 1
    tail = y[panels * rows :]
    pieces = [tail] + [pltpu.roll(tail, 128 - g * stride, axis=1) for g in range(1, folds)]
    last = jnp.concatenate(pieces, axis=0) if folds > 1 else tail
    last = jnp.where(_iota(last.shape, 1) < stride, last, 0.0)
    return jnp.concatenate([y[i * rows : (i + 1) * rows] for i in range(panels)] + [last], axis=1)


def _positions(row, count, span, stride):
    length = row.shape[1]
    rows8 = _up(count, 16)
    holder = _iota((rows8, length), 0)
    hot = (row >= holder * span) & (row < (holder + 1) * span)
    hot_f = hot.astype(F32)
    before = (_iota((length, length), 0) < _iota((length, length), 1)).astype(F32).astype(BF16)
    rank = _dot(hot_f.astype(BF16), before)
    slot = jnp.sum(hot_f * (rank + (holder * stride).astype(F32)), axis=0, keepdims=True)
    base = jnp.sum(hot_f * (holder * span).astype(F32), axis=0, keepdims=True)
    return slot.astype(jnp.int32), row - base.astype(jnp.int32)


def _order(count):
    return sorted(range(1, count), key=lambda o: (min(o, count - o), o))


def _each(count, body, far=False):
    if count <= 17:
        for o in _order(count)[:: -1 if far else 1]:
            body(o)
    else:
        lax.fori_loop(1, count, lambda o, c: (body(o), c)[1], jnp.int32(0))


def moving_kernel(
    n, ncols, width, cap, group,
    right_hbm, left_hbm, updates_hbm, pattern_hbm, targets_hbm, pos_hbm, pivots_hbm,
    parts_hbm, own_hbm, pickt_hbm,
    both_ref, req_out, req_in, hot_ref, pick_out, pick_in, gather_ref, sel_ref, selt_ref, masked_ref, masked_t_ref, con_out, con_in, mov_out, mov_in, part_own,
    s0, r0, s1, r1, s2, r2, s3, r3, s4, r4,
    targets_ref, pos_ref, pivots_ref, right_ref, left_ref, pattern_ref, updates_ref, loaded,
    parts_ref, own_ref, pickt_ref, stored,
):
    loads = [
        pltpu.make_async_copy(src, dst, loaded.at[i])
        for i, (src, dst) in enumerate((
            (targets_hbm, targets_ref), (pos_hbm, pos_ref), (pivots_hbm, pivots_ref),
            (right_hbm, right_ref), (left_hbm, left_ref), (pattern_hbm, pattern_ref),
            (updates_hbm, updates_ref)))
    ]
    for load in loads:
        load.start()
    me = lax.axis_index("rows")
    mycol = lax.axis_index("cols")
    rows_loc, lanes = both_ref.shape
    total = targets_ref.shape[1]
    children, block, _ = updates_ref.shape
    tiles = pattern_ref.shape[1]
    tile = block // tiles

    def to_row(o):
        return lax.rem(me + o, n)

    def from_row(o):
        return lax.rem(me - o + n, n)

    barrier = pltpu.get_barrier_semaphore()
    _each(n, lambda o: pl.semaphore_signal(
        barrier, inc=1, device_id={"rows": to_row(o)}, device_id_type=MESH))
    for o in range(1, ncols):
        pl.semaphore_signal(
            barrier, inc=1, device_id={"cols": lax.rem(mycol + o, ncols)}, device_id_type=MESH)

    def copy(out, into, send, recv, o):
        return pltpu.make_async_remote_copy(
            src_ref=out.at[to_row(o)], dst_ref=into.at[me], send_sem=send.at[o],
            recv_sem=recv.at[o], device_id={"rows": to_row(o)}, device_id_type=MESH)

    def arrival(out, into, send, recv, o):
        return pltpu.make_async_remote_copy(
            src_ref=out.at[to_row(o)], dst_ref=into.at[from_row(o)], send_sem=send.at[o],
            recv_sem=recv.at[o], device_id={"rows": to_row(o)}, device_id_type=MESH)

    half = width // 2
    sides = ((right_ref, 0), (left_ref, half))
    loads[0].wait()
    slot, local = _positions(targets_ref[...], n, rows_loc, cap)
    digits = jnp.where(
        _iota((16, total), 0) < 8, jnp.bitwise_and(local, 255), jnp.right_shift(local, 8))
    digits = digits.astype(F32).astype(BF16)

    def make_request(d, where):
        part = (_iota((cap, total), 0) + d * cap == slot).astype(F32).astype(BF16)
        sel_ref[pl.ds(pl.multiple_of(d * cap, 16), cap), :] = part
        ask = _dot(digits, part, NT)
        where[d, :, :cap] = (ask[:1] + 256.0 * ask[8:9]).astype(jnp.int32)

    _each(n, lambda o: make_request(to_row(o), req_out), far=True)
    pl.semaphore_wait(barrier, n - 1 + ncols - 1)
    _each(n, lambda o: copy(req_out, req_in, s0, r0, o).start(), far=True)
    make_request(me, req_in)
    for load in loads[1:]:
        load.wait()
    chosen = _iota((rows_loc, RANK), 0) == pivots_ref[...]
    pickt_ref[...] = jnp.transpose(chosen.astype(F32)).astype(BF16)
    keep_pickt = pltpu.make_async_copy(pickt_ref, pickt_hbm, stored.at[ncols + 1])
    keep_pickt.start()

    both_ref[...] = functools.reduce(jnp.add, [
        _dot(ref[...],
             (_iota((half, lanes), 1) == _iota((half, lanes), 0) + at).astype(F32).astype(BF16), TN)
        for ref, at in sides]).astype(BF16)
    same = _iota((total, total), 0) == _iota((total, total), 1)
    slot_col = jnp.sum(jnp.where(same, slot.astype(F32), 0.0), axis=1, keepdims=True)
    slot_col = slot_col.astype(jnp.int32)

    def make_selt(d):
        at = _iota((total, cap), 1) + d * cap
        selt_ref[d] = (at == slot_col).astype(F32).astype(BF16)

    make_selt(0)
    _each(n, make_selt)
    for c in range(children):
        for a in range(tiles):
            for b in range(tiles):
                part = updates_ref[c, a * tile : (a + 1) * tile, b * tile : (b + 1) * tile]
                keep = jnp.broadcast_to(pattern_ref[c, a, b], part.shape) != 0
                part = jnp.where(keep, part.astype(F32), 0.0)
                masked_ref[c, a * tile : (a + 1) * tile, b * tile : (b + 1) * tile] = part.astype(BF16)
                masked_t_ref[c, b * tile : (b + 1) * tile, a * tile : (a + 1) * tile] = (
                    jnp.transpose(part).astype(BF16))

    def make_pick(s, where):
        wanted = req_in[s][:, :cap]
        hot = (_iota((rows_loc, cap), 0) == wanted).astype(F32).astype(BF16)
        hot_ref[s] = hot
        where[s] = _pack(_dot(hot, both_ref[...], TN), width).astype(BF16)

    def answer(o):
        arrival(req_out, req_in, s0, r0, n - o).wait_recv()
        make_pick(to_row(o), pick_out)
        copy(pick_out, pick_in, s1, r1, o).start()

    _each(n, answer)
    def fetched(s):
        rows = _unpack(pick_in[s].astype(F32), cap, lanes, width).astype(BF16)
        return _dot(selt_ref[s], rows)

    make_pick(me, pick_in)
    gather_ref[...] = fetched(me)

    def take_rows(o):
        arrival(pick_out, pick_in, s1, r1, o).wait_recv()
        gather_ref[...] += fetched(from_row(o))

    _each(n, take_rows)
    gathered = gather_ref[...].astype(BF16)

    parts = []
    for c in range(children):
        some = gathered[c * block : (c + 1) * block]
        fwd = _dot(masked_ref[c], some)
        trn = _dot(masked_t_ref[c], some)
        parts.append(jnp.where(_iota(fwd.shape, 1) < width // 2, fwd, trn))
    contrib = parts[0] if children == 1 else jnp.concatenate(parts, axis=0)
    code_hi, code_lo = _digits(_encode(contrib, width))

    def make_con(d, where):
        part = sel_ref[pl.ds(pl.multiple_of(d * cap, 16), cap), :]
        moved = _pack(_move_exact(part, code_hi, code_lo), width)
        where[d] = moved.astype(jnp.int32).astype(jnp.int16)

    def send_con(o):
        make_con(to_row(o), con_out)
        copy(con_out, con_in, s2, r2, o).start()

    _each(n, send_con, far=True)
    make_con(me, con_in)

    slot2, place = _positions(pos_ref[...], n, rows_loc, group)
    sel2 = (_iota((n * group, rows_loc), 0) == slot2).astype(F32).astype(BF16)
    diag = _iota((rows_loc, rows_loc), 0) == _iota((rows_loc, rows_loc), 1)
    place_col = jnp.sum(jnp.where(diag, place.astype(F32) + 1.0, 0.0), axis=1, keepdims=True)

    def add_from(s, front):
        code = _unpack(con_in[s].astype(jnp.int32).astype(F32), cap, lanes, width)
        hi, lo = _split2(_decode(code, width))
        hot = hot_ref[s]
        return front + _dot(hot, hi) + _dot(hot, lo)

    front = add_from(me, jnp.zeros((rows_loc, lanes), F32))

    def take(o, front):
        arrival(con_out, con_in, s2, r2, o).wait_recv()
        return add_from(from_row(o), front)

    if n <= 17:
        for o in _order(n):
            front = take(o, front)
    else:
        front = lax.fori_loop(1, n, take, front)

    code = jnp.where(_iota(front.shape, 1) == width + 1, place_col, _encode(front, width))
    moved = _move_exact(sel2, *_digits(code))
    for d in range(n):
        block_d = _pack(moved[d * group : (d + 1) * group], width)
        mov_out[d] = block_d.astype(jnp.int32).astype(jnp.int16)

    def send_moved(o):
        copy(mov_out, mov_in, s3, r3, o).start()

    _each(n, send_moved, far=True)
    mov_in[me] = mov_out[me]
    _each(n, lambda o: arrival(mov_out, mov_in, s3, r3, o).wait_recv())
    got = jnp.concatenate(
        [_unpack(mov_in[d].astype(jnp.int32).astype(F32), group, lanes, width) for d in range(n)],
        axis=0)
    landing = got[:, width + 1 : width + 2].astype(jnp.int32) - 1
    hot2 = (_iota((n * group, rows_loc), 1) == landing).astype(F32).astype(BF16)
    coded = _move_exact(hot2, *_digits(got), TN)
    values = _decode(coded, width)
    hi, lo = _split2(values)
    pickt = pickt_ref[...]
    shi = _dot(pickt, hi).astype(BF16)
    slo = _dot(pickt, lo).astype(BF16)
    part = _dot(shi, hi, NT) + (_dot(shi, lo, NT) + _dot(slo, hi, NT))
    part_own[...] = _encode_part(part * (1.0 / (2.0 * K)), pickt)

    keep_own = pltpu.make_async_copy(own_ref, own_hbm, stored.at[ncols])

    def keep_part(slot):
        return pltpu.make_async_copy(parts_ref.at[slot], parts_hbm.at[slot], stored.at[slot])

    def col_copy(src, slot, to, i):
        return pltpu.make_async_remote_copy(
            src_ref=src, dst_ref=parts_ref.at[slot], send_sem=s4.at[i], recv_sem=r4.at[i],
            device_id={"cols": to}, device_id_type=MESH)

    if ncols == 4:
        across = lax.rem(mycol + 2, 4)
        beside = mycol + 1 - 2 * lax.rem(mycol, 2)
        corner = lax.rem(beside + 2, 4)
        first = col_copy(part_own, mycol, across, 0)
        first.start()
        second = col_copy(part_own, mycol, beside, 1)
        second.start()
        parts_ref[mycol] = part_own[...]
        own_ref[...] = jnp.transpose(values)[:width]
        keep_own.start()
        col_copy(part_own, across, across, 0).wait_recv()
        third = col_copy(parts_ref.at[across], across, beside, 2)
        third.start()
        keep_part(mycol).start()
        keep_part(across).start()
        col_copy(part_own, beside, beside, 1).wait_recv()
        keep_part(beside).start()
        col_copy(part_own, corner, beside, 2).wait_recv()
        keep_part(corner).start()
        col_sends = (first, second, third)
    else:
        col_sends = tuple(
            col_copy(part_own, mycol, lax.rem(mycol + o, ncols), o) for o in range(1, ncols))
        for send in col_sends:
            send.start()
        parts_ref[mycol] = part_own[...]
        own_ref[...] = jnp.transpose(values)[:width]
        keep_own.start()
        for o in range(1, ncols):
            came = lax.rem(mycol - o + ncols, ncols)
            col_copy(part_own, came, came, o).wait_recv()
            keep_part(came).start()
        keep_part(mycol).start()

    for bufs in ((req_out, req_in, s0, r0), (pick_out, pick_in, s1, r1),
                 (con_out, con_in, s2, r2), (mov_out, mov_in, s3, r3)):
        _each(n, lambda o, bufs=bufs: copy(*bufs, o).wait_send())
    for send in col_sends:
        send.wait_send()
    for slot in range(ncols):
        keep_part(slot).wait()
    keep_own.wait()
    keep_pickt.wait()


def _small_inverse(p):
    m = len(p)
    if m == 1:
        return [[1.0 / p[0][0]]]
    if m == 2:
        inv = 1.0 / (p[0][0] * p[1][1] - p[0][1] * p[1][0])
        return [[p[1][1] * inv, -p[0][1] * inv], [-p[1][0] * inv, p[0][0] * inv]]
    h = m // 2

    def mul(a, b):
        return [
            [functools.reduce(jnp.add, [a[i][k] * b[k][j] for k in range(len(b))])
             for j in range(len(b[0]))]
            for i in range(len(a))
        ]

    a = [row[:h] for row in p[:h]]
    b = [row[h:] for row in p[:h]]
    c = [row[:h] for row in p[h:]]
    d = [row[h:] for row in p[h:]]
    ai = _small_inverse(a)
    cai = mul(c, ai)
    aib = mul(ai, b)
    caib = mul(cai, b)
    si = _small_inverse([[d[i][j] - caib[i][j] for j in range(h)] for i in range(h)])
    aibsi = mul(aib, si)
    sicai = mul(si, cai)
    corr = mul(aibsi, cai)
    top = [[ai[i][j] + corr[i][j] for j in range(h)] + [-aibsi[i][j] for j in range(h)]
           for i in range(h)]
    low = [[-sicai[i][j] for j in range(h)] + list(si[i]) for i in range(h)]
    return top + low


def _spd_inverse(gram, step):
    order = gram.shape[0]
    tiles = [gram[i : i + 8] for i in range(0, order, 8)]
    lane = _iota((8, order), 1)
    sub = _iota((8, order), 0)
    lane1 = _iota((1, order), 1)
    for k in range(0, order, step):
        at, off = k // 8, k % 8
        cols = [[jnp.broadcast_to(t[:, k + j : k + j + 1], (8, order)) for j in range(step)]
                for t in tiles]
        pivot = [[cols[at][j][off + i : off + i + 1] for j in range(step)] for i in range(step)]
        binv = _small_inverse(pivot)
        rows = [
            jnp.where((lane1 >= k) & (lane1 < k + step), (lane1 == k + i).astype(F32),
                      tiles[at][off + i : off + i + 1])
            for i in range(step)
        ]
        fresh = [functools.reduce(jnp.add, [binv[i][j] * rows[j] for j in range(step)])
                 for i in range(step)]
        inside = (lane >= k) & (lane < k + step)
        for x in range(len(tiles)):
            t = jnp.where(inside, 0.0, tiles[x])
            for j in range(step):
                t = t - cols[x][j] * fresh[j]
            if x == at:
                for i in range(step):
                    t = jnp.where(sub == off + i, fresh[i], t)
            tiles[x] = t
    return jnp.concatenate(tiles, axis=0)


def _dot3(a, b, dims):
    ah, al = _split2(a)
    bh, bl = _split2(b)
    return _dot(ah, bh, dims) + (_dot(ah, bl, dims) + _dot(al, bh, dims))


LIMIT = 64.0
SETTLED = 1e-5


def _solve_limits():
    limits = []
    for steps in range(4, 9):
        low, high = 1.0, 1e6
        for _ in range(100):
            mid = (low * high) ** 0.5
            rho = (mid - 1.0) / (mid + 1.0)
            for _ in range(steps):
                rho = rho * rho / (2.0 - rho * rho)
            low, high = (mid, high) if rho <= SETTLED else (low, mid)
        limits.append(low)
        if low >= LIMIT:
            break
    return limits


def _left(a):
    return jnp.concatenate(_split2(a), axis=1)


def _right(b):
    both = jnp.concatenate(_split2(b), axis=1)
    return jnp.concatenate([both, both], axis=0)


def _product(left, right):
    both = _dot(left, right)
    half = both.shape[1] // 2
    return both[:, :half] + both[:, half:]


def _narrow(rho):
    scale = 1.0 / (2.0 - rho * rho)
    return 2.0 * scale, rho * rho * scale


def _settling_solve(cross, gram, top):
    order = gram.shape[0]
    bound = jnp.max(top)
    eye = (_iota((order, order), 0) == _iota((order, order), 1)).astype(F32)
    limits = _solve_limits()
    count = 2 + functools.reduce(
        jnp.add, [(bound > limit).astype(jnp.int32) for limit in limits[:-1]])
    inv = 1.0 / (top + 1.0)
    scale, rho = _narrow((top - 1.0) * inv)
    first = 2.0 * inv
    x = (first * scale) * (2.0 * eye - first * gram)
    gram_left = _left(gram)

    def step(_, carry):
        x, rho = carry
        scale, rho = _narrow(rho)
        rest = scale * (2.0 * eye - _product(gram_left, _right(x)))
        return _product(_left(x), _right(rest)), rho

    cross_left = _left(jnp.transpose(cross))
    for _ in range(2):
        x, rho = step(0, (x, rho))
    x, rho = lax.fori_loop(2, count, step, (x, rho))
    right = _right(x)
    scale, rho = _narrow(rho)
    rest = scale * (2.0 * eye - _product(gram_left, right))
    return _product(_left(_product(cross_left, right)), _right(rest))


def leaf_kernel(parts_ref, own_ref, pickt_ref, pivots_ref, fwd_ref, trn_ref, interp_ref):
    ncols = parts_ref.shape[0]
    half = fwd_ref.shape[0]
    fwd_ref[...] = own_ref[:half]
    trn_ref[...] = own_ref[half:]
    cross, diag = 0.0, 0.0
    for c in range(ncols):
        code = parts_ref[c].astype(jnp.int32).astype(F32)
        tail = code[RANK:]
        cross = cross + code[:RANK] * (jnp.exp2(tail[:1]) * (1.0 / QMAX))
        diag = diag + tail[2:3] * (jnp.exp2(tail[1:2]) * (1.0 / QMAX))
    cross = cross + pickt_ref[...].astype(F32) * diag
    pick = (_iota((LEAF, RANK), 0) == pivots_ref[...]).astype(F32).astype(BF16)
    eye = (_iota((RANK, RANK), 0) == _iota((RANK, RANK), 1)).astype(F32)
    hi, lo = _split2(cross)
    gram = _dot(hi, pick) + _dot(lo, pick) + eye
    top = jnp.max(jnp.sum(jnp.abs(gram), axis=1, keepdims=True), axis=0, keepdims=True)
    settles = jnp.max(top) <= LIMIT

    @pl.when(settles)
    def _():
        interp_ref[...] = _settling_solve(cross, gram, top)

    @pl.when(jnp.logical_not(settles))
    def _():
        interp_ref[...] = _dot3(jnp.transpose(cross), _spd_inverse(gram, STEP), ((1,), (0,)))


def per_device(n, ncols, right_sample, left_sample, updates, pattern, targets, cluster_pos, pivots):
    children, block, _ = updates.shape
    rows_loc, half = right_sample.shape
    width = 2 * half
    lanes = _up(width + 2, 128)
    cap = _up(max(2, 3 * children * block // (2 * n)), 16)
    group = _up(rows_loc // n, 16)
    vmem = pl.BlockSpec(memory_space=pltpu.VMEM)
    hbm = pl.BlockSpec(memory_space=pltpu.HBM)
    i16 = jnp.int16
    parts, own, pickt = pl.pallas_call(
        functools.partial(moving_kernel, n, ncols, width, cap, group),
        out_shape=(
            jax.ShapeDtypeStruct((ncols, RANK + 16, LEAF), i16),
            jax.ShapeDtypeStruct((width, rows_loc), F32),
            jax.ShapeDtypeStruct((RANK, LEAF), BF16),
        ),
        in_specs=[hbm] * 7,
        out_specs=(hbm, hbm, hbm),
        scratch_shapes=[
            pltpu.VMEM((rows_loc, lanes), BF16),
            pltpu.VMEM((n, 1, _up(cap, 128)), jnp.int32),
            pltpu.VMEM((n, 1, _up(cap, 128)), jnp.int32),
            pltpu.VMEM((n, rows_loc, cap), BF16),
            pltpu.VMEM((n, _packed(cap, lanes, width), 128), BF16),
            pltpu.VMEM((n, _packed(cap, lanes, width), 128), BF16),
            pltpu.VMEM((children * block, lanes), F32),
            pltpu.VMEM((n * cap, children * block), BF16),
            pltpu.VMEM((n, children * block, cap), BF16),
            pltpu.VMEM(updates.shape, BF16),
            pltpu.VMEM(updates.shape, BF16),
            pltpu.VMEM((n, _packed(cap, lanes, width), 128), i16),
            pltpu.VMEM((n, _packed(cap, lanes, width), 128), i16),
            pltpu.VMEM((n, _packed(group, lanes, width), 128), i16),
            pltpu.VMEM((n, _packed(group, lanes, width), 128), i16),
            pltpu.VMEM((RANK + 16, LEAF), i16),
        ]
        + [pltpu.SemaphoreType.DMA((n,))] * 8
        + [pltpu.SemaphoreType.DMA((ncols,))] * 2
        + [
            pltpu.VMEM((1, children * block), jnp.int32),
            pltpu.VMEM((1, rows_loc), jnp.int32),
            pltpu.VMEM(pivots.shape, jnp.int32),
            pltpu.VMEM((half, rows_loc), BF16),
            pltpu.VMEM((half, rows_loc), BF16),
            pltpu.SMEM(pattern.shape, jnp.int32),
            pltpu.VMEM(updates.shape, BF16),
            pltpu.SemaphoreType.DMA((7,)),
            pltpu.VMEM((ncols, RANK + 16, LEAF), i16),
            pltpu.VMEM((width, rows_loc), F32),
            pltpu.VMEM((RANK, LEAF), BF16),
            pltpu.SemaphoreType.DMA((ncols + 2,)),
        ],
        compiler_params=pltpu.CompilerParams(collective_id=0, has_side_effects=True),
        name="moving",
    )(right_sample.T, left_sample.T, updates, pattern, targets.reshape(1, -1), cluster_pos.reshape(1, -1), pivots)
    forward, transposed, interp = pl.pallas_call(
        leaf_kernel,
        out_shape=(
            jax.ShapeDtypeStruct((half, rows_loc), F32),
            jax.ShapeDtypeStruct((half, rows_loc), F32),
            jax.ShapeDtypeStruct((rows_loc, RANK), F32),
        ),
        in_specs=[vmem] * 4,
        out_specs=(vmem, vmem, vmem),
        name="leaf",
    )(parts, own, pickt, pivots)
    return forward.T, transposed.T, interp


def solution(mesh):
    sizes = dict(mesh.shape)
    return jax.shard_map(
        functools.partial(per_device, sizes["rows"], sizes["cols"]),
        mesh=mesh,
        in_specs=(
            P("rows", "cols"),
            P("rows", "cols"),
            P("rows", None, None),
            P("rows", None, None),
            P("rows", None),
            P("rows"),
            P("rows", None),
        ),
        out_specs=(P("rows", "cols"), P("rows", "cols"), P("rows", None)),
        check_vma=False,
    )
```
